128 devices in a mesh: gx: 32 (over y, z, core), gy: 4 (over x).
Axes of the slice: x: 4, y: 4, z: 4, core: 2. Of those that a mesh axis runs over, the one named last changes fastest.
Arguments:
- hamiltonian: bfloat16 [128, 16, 64, 576], P('gx', 'gy'), as said below
- density: bfloat16 [128, 16, 64, 576], P('gx', 'gy'), as said below
- block_pattern: int32 [128, 16, 9], P('gx', 'gy'), may hold values from 0 to 1, as said below
- filter_mask: int32 [128, 16, 9], P('gx', 'gy'), may hold values from 0 to 1, as said below
Outputs:
- gradient: bfloat16 [128, 16, 64, 576], P('gx', 'gy')
The draws below stay inside these ranges and needn't reach their ends.
Inputs may be any that keep to these rules, and one draw needn't show every extreme that they name: `block_pattern`: Symmetric: the value at block row i and slot k equals the value at block row i + s_k and slot 8 - k; the middle slot (k = 4) is always 1. `filter_mask`: Symmetric: the value at block row i and slot k equals the value at block row i + s_k and slot 8 - k; the middle slot (k = 4) is always 1. `hamiltonian`: A symmetric matrix: block (i, k) is the transpose of block (i + s_k, 8 - k), and every middle block (k = 4) is symmetric. `density`: A symmetric matrix: block (i, k) is the transpose of block (i + s_k, 8 - k), and every middle block (k = 4) is symmetric.
All inputs are finite; a program needn't handle non-finite values.
Results may differ from the reference program's by a relative error of at most 0.006.
Values may be sent and summed in bfloat16 or wider, within the bound.
A program may use at most 192 MiB of HBM per device.

```python
import jax
import jax.numpy as jnp

BS = 64
GXB = 128
GYB = 16


def symmetric_mask(key, salt):
    base = jax.random.randint(jax.random.fold_in(key, salt), (GXB, GYB, 9), 0, 4)
    live = (base != 0).astype(jnp.int32)
    columns = []
    for slot_index in range(9):
        if slot_index == 4:
            columns.append(jnp.ones((GXB, GYB), jnp.int32))
        elif slot_index > 4:
            columns.append(live[:, :, slot_index])
        else:
            shift_x = slot_index // 3 - 1
            shift_y = slot_index % 3 - 1
            columns.append(jnp.roll(live[:, :, 8 - slot_index], (-shift_x, -shift_y), axis=(0, 1)))
    return jnp.stack(columns, axis=-1)


def symmetric_strips(key, scale, limit):
    shape = (GXB, GYB, BS, 9 * BS)
    base = jax.random.normal(key, shape, jnp.float32)
    base = jnp.clip(base * scale, -limit, limit)
    blocks = base.reshape(GXB, GYB, BS, 9, BS)
    columns = []
    for slot_index in range(9):
        if slot_index == 4:
            middle = blocks[:, :, :, 4, :]
            columns.append((middle + jnp.swapaxes(middle, 2, 3)) * 0.5)
        elif slot_index > 4:
            columns.append(blocks[:, :, :, slot_index, :])
        else:
            shift_x = slot_index // 3 - 1
            shift_y = slot_index % 3 - 1
            source = blocks[:, :, :, 8 - slot_index, :]
            moved = jnp.roll(source, (-shift_x, -shift_y), axis=(0, 1))
            columns.append(jnp.swapaxes(moved, 2, 3))
    return jnp.stack(columns, axis=3).reshape(shape)


def draw_hamiltonian(key, part):
    return symmetric_strips(jax.random.fold_in(key, 31), 0.4, 2.5).astype(jnp.bfloat16)


def draw_density(key, part):
    scale = (3.0 * BS) ** (-0.5)
    return symmetric_strips(jax.random.fold_in(key, 47), scale, 6.0 * scale).astype(jnp.bfloat16)


def draw_block_pattern(key, part):
    return symmetric_mask(key, 11)


def draw_filter_mask(key, part):
    return symmetric_mask(key, 23)


def setup_inputs(seed: int = 0) -> dict:
    keys = jax.random.split(jax.random.key(seed), 5)
    return {
        "hamiltonian": draw_hamiltonian(jax.random.fold_in(keys[4], 71), 0),
        "density": draw_density(jax.random.fold_in(keys[4], 71), 0),
        "block_pattern": draw_block_pattern(jax.random.fold_in(keys[4], 71), 0),
        "filter_mask": draw_filter_mask(jax.random.fold_in(keys[4], 71), 0),
    }


def pair_list(target):
    target_x = target // 3 - 1
    target_y = target % 3 - 1
    pairs = []
    for source in range(9):
        move_x = source // 3 - 1
        move_y = source % 3 - 1
        rest_x = target_x - move_x
        rest_y = target_y - move_y
        if abs(rest_x) <= 1 and abs(rest_y) <= 1:
            pairs.append((source, (rest_x + 1) * 3 + rest_y + 1, move_x, move_y))
    return pairs


def block_mask(strips, mask, width):
    shape = strips.shape
    split = strips.reshape(shape[0], shape[1], width, 9, width)
    split = split * mask[:, :, None, :, None].astype(strips.dtype)
    return split.reshape(shape)


def stencil_product(left, right, margin, width):
    rows_x = left.shape[0]
    rows_y = left.shape[1]
    outputs = []
    for target in range(9):
        lefts = []
        rights = []
        for source, inner, move_x, move_y in pair_list(target):
            lefts.append(left[:, :, :, source * width:(source + 1) * width])
            moved = right[margin + move_x:margin + move_x + rows_x, margin + move_y:margin + move_y + rows_y]
            rights.append(moved[:, :, :, inner * width:(inner + 1) * width])
        joined_left = jnp.concatenate(lefts, axis=-1).astype(jnp.float32)
        joined_right = jnp.concatenate(rights, axis=-2).astype(jnp.float32)
        outputs.append(jnp.einsum("xyab,xybc->xyac", joined_left, joined_right))
    return jnp.concatenate(outputs, axis=-1)


def wrap_pad(strips):
    return jnp.pad(strips, ((1, 1), (1, 1), (0, 0), (0, 0)), mode="wrap")


def transposed(padded, rows_x, rows_y, width):
    blocks = []
    for target in range(9):
        move_x = target // 3 - 1
        move_y = target % 3 - 1
        moved = padded[1 + move_x:1 + move_x + rows_x, 1 + move_y:1 + move_y + rows_y]
        piece = moved[:, :, :, (8 - target) * width:(9 - target) * width]
        blocks.append(jnp.swapaxes(piece, 2, 3))
    return jnp.concatenate(blocks, axis=-1)


def reference(hamiltonian, density, block_pattern, filter_mask):
    width = BS
    rows_x = hamiltonian.shape[0]
    rows_y = hamiltonian.shape[1]
    ham_masked = block_mask(hamiltonian, block_pattern, width)
    dens_masked = block_mask(density, block_pattern, width)
    dens_pad = wrap_pad(dens_masked)
    hp = block_mask(stencil_product(ham_masked, dens_pad, 1, width), filter_mask, width).astype(jnp.bfloat16)
    hpp = block_mask(stencil_product(hp, dens_pad, 1, width), filter_mask, width).astype(jnp.bfloat16)
    hp_pad = wrap_pad(hp)
    php = block_mask(stencil_product(dens_masked, hp_pad, 1, width), filter_mask, width)
    hp_turned = transposed(hp_pad, rows_x, rows_y, width)
    hpp_turned = transposed(wrap_pad(hpp), rows_x, rows_y, width)
    linear = hp.astype(jnp.float32) + hp_turned.astype(jnp.float32)
    cubic = hpp.astype(jnp.float32) + php + hpp_turned.astype(jnp.float32)
    total = block_mask(3.0 * linear - 2.0 * cubic, filter_mask, width)
    return total.astype(jnp.bfloat16)
```

```python
import functools

import jax
import jax.numpy as jnp
from jax import lax
from jax.experimental import pallas as pl
from jax.experimental.pallas import tpu as pltpu
from jax.sharding import PartitionSpec as P

TILE = 256
LANES = 3 * TILE
MESH = pl.DeviceIdType.MESH
SIDES = ((1, 0), (-1, 0), (0, 1), (0, -1), (1, 1), (1, -1), (-1, 1), (-1, -1))


def halo_parts(sx, sy):
    from_x = {1: pl.ds(4, 1), -1: pl.ds(1, 1), 0: pl.ds(1, 4)}[sx]
    to_x = {1: pl.ds(0, 1), -1: pl.ds(5, 1), 0: pl.ds(1, 4)}[sx]
    from_y = {1: pl.ds(4, 1), -1: pl.ds(1, 1), 0: pl.ds(1, 4)}[sy]
    to_y = {1: pl.ds(0, 1), -1: pl.ds(5, 1), 0: pl.ds(1, 4)}[sy]
    tiles = {1: (1, 2), -1: (0, 1), 0: (0, 1, 2)}[sx]
    if sy == 0:
        lanes = [(TILE * tiles[0], TILE * len(tiles))]
    else:
        lanes = [(TILE * t + (128 if sy == 1 else 0), 128) for t in tiles]
    return [
        ((from_x, from_y, slice(None), pl.ds(start, size)), (to_x, to_y, slice(None), pl.ds(start, size)))
        for start, size in lanes
    ]


COPIES = sum(len(halo_parts(sx, sy)) for sx, sy in SIDES)


def kernel(
    nx, ny, ham, den, pat, fil, out,
    raw_h, raw_d, pat_row, fil_row, e_h, e_d, e_s, hp, total, result,
    load_sem, store_sem, send_sem, recv_sem,
):
    gx = lax.axis_index("gx")
    gy = lax.axis_index("gy")

    def device(sx, sy):
        return (lax.rem(gx + (sx + nx), nx), lax.rem(gy + (sy + ny), ny))

    load_d = pltpu.make_async_copy(den, raw_d, load_sem.at[0])
    load_h = pltpu.make_async_copy(ham, raw_h, load_sem.at[1])
    load_d.start()
    load_h.start()

    barrier = pltpu.get_barrier_semaphore()
    for sx, sy in SIDES:
        pl.semaphore_signal(barrier, inc=1, device_id=device(sx, sy), device_id_type=MESH)

    row = lax.broadcasted_iota(jnp.int32, (4, LANES), 0)
    lane = lax.broadcasted_iota(jnp.int32, (4, LANES), 1)
    place = ((lane >> 6) & 3) - (row & 1)
    slot = jnp.where((place >= 0) & (place <= 2), 3 * (lane >> 8) + place, 9)
    for x in range(4):
        for source, target in ((pat, pat_row), (fil, fil_row)):
            spread = jnp.zeros((4, LANES), jnp.int32)
            for k in range(9):
                spread = jnp.where(slot == k, source[x, :, k : k + 1], spread)
            target[x] = spread.astype(jnp.float32)

    def spread_strips(raw, e):
        def body(step, carry):
            x = step // 2
            p = step % 2
            gap = jnp.zeros((64, 64), jnp.bfloat16)
            v = raw[x, 2 * p]
            m = pat_row[x, pl.ds(2 * p, 1), :].astype(jnp.bfloat16)
            e[x + 1, 2 * p + 1, :, 0:256] = v[:, 0:256] * m[:, 0:256]
            e[x + 1, 2 * p + 1, :, 256:512] = v[:, 192:448] * m[:, 256:512]
            e[x + 1, 2 * p + 1, :, 512:768] = (
                jnp.concatenate([v[:, 384:576], gap], axis=1) * m[:, 512:768]
            )
            v = raw[x, 2 * p + 1]
            m = pat_row[x, pl.ds(2 * p + 1, 1), :].astype(jnp.bfloat16)
            e[x + 1, 2 * p + 2, :, 0:256] = (
                jnp.concatenate([gap, v[:, 0:192]], axis=1) * m[:, 0:256]
            )
            e[x + 1, 2 * p + 2, :, 256:512] = v[:, 128:384] * m[:, 256:512]
            e[x + 1, 2 * p + 2, :, 512:768] = v[:, 320:576] * m[:, 512:768]
            return carry

        lax.fori_loop(0, 8, body, 0)

    def copies(e, base):
        made = []
        for sx, sy in SIDES:
            for source, target in halo_parts(sx, sy):
                made.append(
                    pltpu.make_async_remote_copy(
                        src_ref=e.at[source],
                        dst_ref=e.at[target],
                        send_sem=send_sem.at[base + len(made)],
                        recv_sem=recv_sem.at[base + len(made)],
                        device_id=device(sx, sy),
                        device_id_type=MESH,
                    )
                )
        return made

    copies_d = copies(e_d, 0)
    copies_h = copies(e_h, COPIES)
    copies_s = copies(e_s, 2 * COPIES)

    load_d.wait()
    spread_strips(raw_d, e_d)
    pl.semaphore_wait(barrier, len(SIDES))
    for copy in copies_d:
        copy.start()
    load_h.wait()
    spread_strips(raw_h, e_h)
    for copy in copies_h:
        copy.start()

    hole = jnp.zeros((64, 128), jnp.bfloat16)

    def product(left, e, x, p, target):
        low = max(target - 1, 0)
        high = min(target + 1, 2)
        rights = []
        for source in range(low, high + 1):
            start = TILE * (target - source + 1)
            first = e[x + source, 2 * p, :, start + 128 : start + 256]
            second = e[x + source, 2 * p + 1, :, start : start + 256]
            third = e[x + source, 2 * p + 2, :, start : start + 256]
            fourth = e[x + source, 2 * p + 3, :, start : start + 128]
            rights.append(jnp.concatenate([first, hole], axis=1))
            rights.append(second)
            rights.append(third)
            rights.append(jnp.concatenate([hole, fourth], axis=1))
        a = left[:, :, TILE * low : TILE * (high + 1)]
        a = a.reshape(128, TILE * (high + 1 - low))
        b = jnp.concatenate(rights, axis=0)
        return jnp.dot(a, b, preferred_element_type=jnp.float32)

    def filter_of(x, p, target):
        even = fil_row[x, pl.ds(2 * p, 1), TILE * target : TILE * (target + 1)]
        odd = fil_row[x, pl.ds(2 * p + 1, 1), TILE * target : TILE * (target + 1)]
        return jnp.concatenate(
            [jnp.broadcast_to(even, (64, TILE)), jnp.broadcast_to(odd, (64, TILE))], axis=0
        )

    def pair(step):
        return step // 2, step % 2

    def hp_body(step, carry):
        x, p = pair(step)
        left = e_h[x + 1, pl.ds(2 * p + 1, 2)]
        for target in range(3):
            value = product(left, e_d, x, p, target) * filter_of(x, p, target)
            hp[x, pl.ds(2 * p, 2), :, TILE * target : TILE * (target + 1)] = value.astype(
                jnp.bfloat16
            ).reshape(2, 64, TILE)
        return carry

    def sum_body(step, carry):
        x, p = pair(step)
        left = e_d[x + 1, pl.ds(2 * p + 1, 2)]
        for target in range(3):
            lanes = slice(TILE * target, TILE * (target + 1))
            turned = product(left, e_h, x, p, target) * filter_of(x, p, target)
            turned = turned.astype(jnp.bfloat16).astype(jnp.float32)
            both = turned + hp[x, pl.ds(2 * p, 2), :, lanes].reshape(128, TILE).astype(jnp.float32)
            total[x, pl.ds(2 * p, 2), :, lanes] = (3.0 * both).reshape(2, 64, TILE)
            e_s[x + 1, pl.ds(2 * p + 1, 2), :, lanes] = both.astype(jnp.bfloat16).reshape(
                2, 64, TILE
            )
        return carry

    def hpp_body(step, carry):
        x, p = pair(step)
        left = hp[x, pl.ds(2 * p, 2)]
        for target in range(3):
            lanes = slice(TILE * target, TILE * (target + 1))
            value = product(left, e_d, x, p, target).reshape(2, 64, TILE)
            total[x, pl.ds(2 * p, 2), :, lanes] = (
                total[x, pl.ds(2 * p, 2), :, lanes] - 2.0 * value
            )
        return carry

    def store(x):
        return pltpu.make_async_copy(result.at[x], out.at[x], store_sem.at[x])

    def last_body(x, carry):
        for p in range(2):
            left = e_d[x + 1, pl.ds(2 * p + 1, 2)]
            parts = []
            for target in range(3):
                lanes = slice(TILE * target, TILE * (target + 1))
                value = product(left, e_s, x, p, target)
                value = total[x, pl.ds(2 * p, 2), :, lanes].reshape(128, TILE) - 2.0 * value
                parts.append((value * filter_of(x, p, target)).astype(jnp.bfloat16))
            result[x, 2 * p] = jnp.concatenate([part[0:64, 0:192] for part in parts], axis=1)
            result[x, 2 * p + 1] = jnp.concatenate(
                [part[64:128, 64:256] for part in parts], axis=1
            )
        return carry

    for copy in copies_d:
        copy.wait_recv()
    lax.fori_loop(0, 8, hp_body, 0)
    for copy in copies_h:
        copy.wait_recv()
    lax.fori_loop(0, 8, sum_body, 0)
    for copy in copies_s:
        copy.start()
    lax.fori_loop(0, 8, hpp_body, 0)
    for copy in copies_s:
        copy.wait_recv()
    lax.fori_loop(0, 4, last_body, 0)
    for x in range(4):
        store(x).start()
    for copy in copies_d + copies_h + copies_s:
        copy.wait_send()
    for x in range(4):
        store(x).wait()


def per_device(nx, ny, hamiltonian, density, block_pattern, filter_mask):
    shape = hamiltonian.shape
    ring = (6, 6, 64, LANES)
    vmem = pl.BlockSpec(memory_space=pltpu.VMEM)
    anywhere = pl.BlockSpec(memory_space=pl.ANY)
    return pl.pallas_call(
        functools.partial(kernel, nx, ny),
        out_shape=jax.ShapeDtypeStruct(shape, jnp.bfloat16),
        in_specs=[anywhere, anywhere, vmem, vmem],
        out_specs=anywhere,
        scratch_shapes=[
            pltpu.VMEM(shape, jnp.bfloat16),
            pltpu.VMEM(shape, jnp.bfloat16),
            pltpu.VMEM((4, 4, LANES), jnp.float32),
            pltpu.VMEM((4, 4, LANES), jnp.float32),
            pltpu.VMEM(ring, jnp.bfloat16),
            pltpu.VMEM(ring, jnp.bfloat16),
            pltpu.VMEM(ring, jnp.bfloat16),
            pltpu.VMEM((4, 4, 64, LANES), jnp.bfloat16),
            pltpu.VMEM((4, 4, 64, LANES), jnp.float32),
            pltpu.VMEM(shape, jnp.bfloat16),
            pltpu.SemaphoreType.DMA((2,)),
            pltpu.SemaphoreType.DMA((4,)),
            pltpu.SemaphoreType.DMA((3 * COPIES,)),
            pltpu.SemaphoreType.DMA((3 * COPIES,)),
        ],
        compiler_params=pltpu.CompilerParams(collective_id=0, has_side_effects=True),
    )(hamiltonian, density, block_pattern, filter_mask)


def solution(mesh):
    return jax.shard_map(
        functools.partial(per_device, mesh.shape["gx"], mesh.shape["gy"]),
        mesh=mesh,
        in_specs=(
            P("gx", "gy", None, None),
            P("gx", "gy", None, None),
            P("gx", "gy", None),
            P("gx", "gy", None),
        ),
        out_specs=P("gx", "gy", None, None),
        check_vma=False,
    )
```

```python
import functools

import jax
import jax.numpy as jnp
from jax import lax
from jax.experimental import pallas as pl
from jax.experimental.pallas import tpu as pltpu
from jax.sharding import PartitionSpec as P

TILE = 256
LANES = 3 * TILE
MESH = pl.DeviceIdType.MESH
SIDES = ((1, 1), (1, -1), (-1, 1), (-1, -1), (0, 1), (0, -1), (1, 0), (-1, 0))


def halo_parts(sx, sy):
    whole = slice(None)
    from_x = {1: pl.ds(4, 1), -1: pl.ds(1, 1), 0: pl.ds(1, 4)}[sx]
    to_x = {1: pl.ds(0, 1), -1: pl.ds(5, 1), 0: pl.ds(1, 4)}[sx]
    from_y = {1: pl.ds(4, 1), -1: pl.ds(1, 1), 0: pl.ds(1, 4)}[sy]
    to_y = {1: pl.ds(0, 1), -1: pl.ds(5, 1), 0: pl.ds(1, 4)}[sy]
    half = 128 if sy == 1 else 0
    if sy == 0:
        parts = [(from_x, to_x, TILE, TILE)]
    elif sx != 0:
        parts = [(from_x, to_x, TILE + half, 128)]
    else:
        first = pl.ds(1, 1)
        parts = [
            (first, first, half, 128),
            (from_x, to_x, 2 * TILE + half, 128),
            (from_x, to_x, TILE + half, 128),
        ]
    return [
        ((a, from_y, whole, pl.ds(start, size)), (b, to_y, whole, pl.ds(start, size)))
        for a, b, start, size in parts
    ]


COPIES = sum(len(halo_parts(sx, sy)) for sx, sy in SIDES)


def turn_dense(e, x, y, tile):
    at = TILE * tile
    pile = jnp.concatenate([e[x, y, :, at + 128 : at + 256], e[x, y + 1, :, at : at + 128]], axis=0)
    return pile.T


def fill_inner(e):
    for x, ring, tile in ((1, 0, 0), (4, 5, 2)):
        here, there = TILE * tile, TILE * (2 - tile)
        turned = turn_dense(e, x, 2, tile)
        e[ring, 2, :, there + 128 : there + 256] = turned[0:64]
        e[ring, 3, :, there : there + 128] = turned[64:128]
        for y in (2, 4):
            pile = jnp.concatenate(
                [e[x, y, :, here : here + 128], e[x, y - 1, :, here + 128 : here + 256]], axis=0
            )
            turned = pile.T
            e[ring, y, :, there : there + 128] = turned[0:64]
            e[ring, y - 1, :, there + 128 : there + 256] = turned[64:128]


def fill_outer(e):
    for x, ring, tile in ((1, 0, 0), (4, 5, 2)):
        there = TILE * (2 - tile)
        for y in (0, 4):
            turned = turn_dense(e, x, y, tile)
            e[ring, y, :, there + 128 : there + 256] = turned[0:64]
            e[ring, y + 1, :, there : there + 128] = turned[64:128]
    for x in (2, 3, 4):
        e[x, 0, :, 128:256] = turn_dense(e, x - 1, 0, 2)[0:64]
        e[x, 5, :, 0:128] = turn_dense(e, x - 1, 4, 2)[64:128]


def kernel(
    nx, ny, ham, den, pat, fil, out,
    raw_h, raw_d, pat_row, fil_row, e_h, e_d, e_s, hp, total, result,
    load_sem, store_sem, send_sem, recv_sem,
):
    gx = lax.axis_index("gx")
    gy = lax.axis_index("gy")

    def device(sx, sy):
        return (lax.rem(gx + (sx + nx), nx), lax.rem(gy + (sy + ny), ny))

    load_d = pltpu.make_async_copy(den, raw_d, load_sem.at[0])
    load_h = pltpu.make_async_copy(ham, raw_h, load_sem.at[1])
    load_d.start()
    load_h.start()

    barrier = pltpu.get_barrier_semaphore()
    for sx, sy in SIDES:
        pl.semaphore_signal(barrier, inc=1, device_id=device(sx, sy), device_id_type=MESH)

    row = lax.broadcasted_iota(jnp.int32, (4, LANES), 0)
    lane = lax.broadcasted_iota(jnp.int32, (4, LANES), 1)
    place = ((lane >> 6) & 3) - (row & 1)
    slot = jnp.where((place >= 0) & (place <= 2), 3 * (lane >> 8) + place, 9)
    for x in range(4):
        for source, target in ((pat, pat_row), (fil, fil_row)):
            spread = jnp.zeros((4, LANES), jnp.int32)
            for k in range(9):
                spread = jnp.where(slot == k, source[x, :, k : k + 1], spread)
            target[x] = spread.astype(jnp.float32)

    def spread_strips(raw, e):
        def body(step, carry):
            x = step // 2
            p = step % 2
            gap = jnp.zeros((64, 64), jnp.bfloat16)
            v = raw[x, 2 * p]
            m = pat_row[x, pl.ds(2 * p, 1), :].astype(jnp.bfloat16)
            e[x + 1, 2 * p + 1, :, 0:256] = v[:, 0:256] * m[:, 0:256]
            e[x + 1, 2 * p + 1, :, 256:512] = v[:, 192:448] * m[:, 256:512]
            e[x + 1, 2 * p + 1, :, 512:768] = (
                jnp.concatenate([v[:, 384:576], gap], axis=1) * m[:, 512:768]
            )
            v = raw[x, 2 * p + 1]
            m = pat_row[x, pl.ds(2 * p + 1, 1), :].astype(jnp.bfloat16)
            e[x + 1, 2 * p + 2, :, 0:256] = (
                jnp.concatenate([gap, v[:, 0:192]], axis=1) * m[:, 0:256]
            )
            e[x + 1, 2 * p + 2, :, 256:512] = v[:, 128:384] * m[:, 256:512]
            e[x + 1, 2 * p + 2, :, 512:768] = v[:, 320:576] * m[:, 512:768]
            return carry

        lax.fori_loop(0, 8, body, 0)

    def copies(e, base):
        made = []
        for sx, sy in SIDES:
            for source, target in halo_parts(sx, sy):
                made.append(
                    pltpu.make_async_remote_copy(
                        src_ref=e.at[source],
                        dst_ref=e.at[target],
                        send_sem=send_sem.at[base + len(made)],
                        recv_sem=recv_sem.at[base + len(made)],
                        device_id=device(sx, sy),
                        device_id_type=MESH,
                    )
                )
        return made

    copies_d = copies(e_d, 0)
    copies_h = copies(e_h, COPIES)
    copies_s = copies(e_s, 2 * COPIES)

    load_d.wait()
    spread_strips(raw_d, e_d)
    pl.semaphore_wait(barrier, len(SIDES))
    for copy in copies_d:
        copy.start()
    load_h.wait()
    spread_strips(raw_h, e_h)
    for copy in copies_h:
        copy.start()
    fill_inner(e_d)
    fill_inner(e_h)

    hole = jnp.zeros((64, 128), jnp.bfloat16)

    def product(left, e, x, p, target):
        low = max(target - 1, 0)
        high = min(target + 1, 2)
        rights = []
        for source in range(low, high + 1):
            start = TILE * (target - source + 1)
            first = e[x + source, 2 * p, :, start + 128 : start + 256]
            second = e[x + source, 2 * p + 1, :, start : start + 256]
            third = e[x + source, 2 * p + 2, :, start : start + 256]
            fourth = e[x + source, 2 * p + 3, :, start : start + 128]
            rights.append(jnp.concatenate([first, hole], axis=1))
            rights.append(second)
            rights.append(third)
            rights.append(jnp.concatenate([hole, fourth], axis=1))
        a = left[:, :, TILE * low : TILE * (high + 1)]
        a = a.reshape(128, TILE * (high + 1 - low))
        b = jnp.concatenate(rights, axis=0)
        return jnp.dot(a, b, preferred_element_type=jnp.float32)

    def filter_of(x, p, target):
        even = fil_row[x, pl.ds(2 * p, 1), TILE * target : TILE * (target + 1)]
        odd = fil_row[x, pl.ds(2 * p + 1, 1), TILE * target : TILE * (target + 1)]
        return jnp.concatenate(
            [jnp.broadcast_to(even, (64, TILE)), jnp.broadcast_to(odd, (64, TILE))], axis=0
        )

    def pair(step):
        return step // 2, step % 2

    def hp_body(step, carry):
        x, p = pair(step)
        left = e_h[x + 1, pl.ds(2 * p + 1, 2)]
        for target in range(3):
            value = product(left, e_d, x, p, target) * filter_of(x, p, target)
            hp[x, pl.ds(2 * p, 2), :, TILE * target : TILE * (target + 1)] = value.astype(
                jnp.bfloat16
            ).reshape(2, 64, TILE)
        return carry

    def sum_body(step, carry):
        x, p = pair(step)
        left = e_d[x + 1, pl.ds(2 * p + 1, 2)]
        for target in range(3):
            lanes = slice(TILE * target, TILE * (target + 1))
            turned = product(left, e_h, x, p, target) * filter_of(x, p, target)
            turned = turned.astype(jnp.bfloat16).astype(jnp.float32)
            both = turned + hp[x, pl.ds(2 * p, 2), :, lanes].reshape(128, TILE).astype(jnp.float32)
            total[x, pl.ds(2 * p, 2), :, lanes] = (3.0 * both).reshape(2, 64, TILE)
            e_s[x + 1, pl.ds(2 * p + 1, 2), :, lanes] = both.astype(jnp.bfloat16).reshape(
                2, 64, TILE
            )
        return carry

    def hpp_body(step, carry):
        x, p = pair(step)
        left = hp[x, pl.ds(2 * p, 2)]
        for target in range(3):
            lanes = slice(TILE * target, TILE * (target + 1))
            value = product(left, e_d, x, p, target).reshape(2, 64, TILE)
            total[x, pl.ds(2 * p, 2), :, lanes] = (
                total[x, pl.ds(2 * p, 2), :, lanes] - 2.0 * value
            )
        return carry

    def store(x):
        return pltpu.make_async_copy(result.at[x], out.at[x], store_sem.at[x])

    def last_body(x, carry):
        for p in range(2):
            left = e_d[x + 1, pl.ds(2 * p + 1, 2)]
            parts = []
            for target in range(3):
                lanes = slice(TILE * target, TILE * (target + 1))
                value = product(left, e_s, x, p, target)
                value = total[x, pl.ds(2 * p, 2), :, lanes].reshape(128, TILE) - 2.0 * value
                parts.append((value * filter_of(x, p, target)).astype(jnp.bfloat16))
            result[x, 2 * p] = jnp.concatenate([part[0:64, 0:192] for part in parts], axis=1)
            result[x, 2 * p + 1] = jnp.concatenate(
                [part[64:128, 64:256] for part in parts], axis=1
            )
        return carry

    for copy in copies_d:
        copy.wait_recv()
    fill_outer(e_d)
    lax.fori_loop(0, 8, hp_body, 0)
    for copy in copies_h:
        copy.wait_recv()
    fill_outer(e_h)
    lax.fori_loop(0, 8, sum_body, 0)
    for copy in copies_s:
        copy.start()
    fill_inner(e_s)
    lax.fori_loop(0, 8, hpp_body, 0)
    for copy in copies_s:
        copy.wait_recv()
    fill_outer(e_s)
    lax.fori_loop(0, 4, last_body, 0)
    for x in range(4):
        store(x).start()
    for copy in copies_d + copies_h + copies_s:
        copy.wait_send()
    for x in range(4):
        store(x).wait()


def per_device(nx, ny, hamiltonian, density, block_pattern, filter_mask):
    shape = hamiltonian.shape
    ring = (6, 6, 64, LANES)
    vmem = pl.BlockSpec(memory_space=pltpu.VMEM)
    anywhere = pl.BlockSpec(memory_space=pl.ANY)
    return pl.pallas_call(
        functools.partial(kernel, nx, ny),
        out_shape=jax.ShapeDtypeStruct(shape, jnp.bfloat16),
        in_specs=[anywhere, anywhere, vmem, vmem],
        out_specs=anywhere,
        scratch_shapes=[
            pltpu.VMEM(shape, jnp.bfloat16),
            pltpu.VMEM(shape, jnp.bfloat16),
            pltpu.VMEM((4, 4, LANES), jnp.float32),
            pltpu.VMEM((4, 4, LANES), jnp.float32),
            pltpu.VMEM(ring, jnp.bfloat16),
            pltpu.VMEM(ring, jnp.bfloat16),
            pltpu.VMEM(ring, jnp.bfloat16),
            pltpu.VMEM((4, 4, 64, LANES), jnp.bfloat16),
            pltpu.VMEM((4, 4, 64, LANES), jnp.float32),
            pltpu.VMEM(shape, jnp.bfloat16),
            pltpu.SemaphoreType.DMA((2,)),
            pltpu.SemaphoreType.DMA((4,)),
            pltpu.SemaphoreType.DMA((3 * COPIES,)),
            pltpu.SemaphoreType.DMA((3 * COPIES,)),
        ],
        compiler_params=pltpu.CompilerParams(collective_id=0, has_side_effects=True),
    )(hamiltonian, density, block_pattern, filter_mask)


def solution(mesh):
    return jax.shard_map(
        functools.partial(per_device, mesh.shape["gx"], mesh.shape["gy"]),
        mesh=mesh,
        in_specs=(
            P("gx", "gy", None, None),
            P("gx", "gy", None, None),
            P("gx", "gy", None),
            P("gx", "gy", None),
        ),
        out_specs=P("gx", "gy", None, None),
        check_vma=False,
    )
```

```python
import functools

import jax
import jax.numpy as jnp
from jax import lax
from jax.experimental import pallas as pl
from jax.experimental.pallas import tpu as pltpu
from jax.sharding import PartitionSpec as P

TILE = 256
LANES = 3 * TILE
MESH = pl.DeviceIdType.MESH
SIDES = ((1, 1), (1, -1), (-1, 1), (-1, -1), (0, 1), (0, -1), (1, 0), (-1, 0))


def halo_parts(sx, sy):
    whole = slice(None)
    from_x = {1: pl.ds(4, 1), -1: pl.ds(1, 1), 0: pl.ds(1, 4)}[sx]
    to_x = {1: pl.ds(0, 1), -1: pl.ds(5, 1), 0: pl.ds(1, 4)}[sx]
    from_y = {1: pl.ds(4, 1), -1: pl.ds(1, 1), 0: pl.ds(1, 4)}[sy]
    to_y = {1: pl.ds(0, 1), -1: pl.ds(5, 1), 0: pl.ds(1, 4)}[sy]
    half = 128 if sy == 1 else 0
    if sy == 0:
        parts = [(from_x, to_x, TILE, TILE)]
    elif sx != 0:
        parts = [(from_x, to_x, TILE + half, 128)]
    else:
        first = pl.ds(1, 1)
        parts = [
            (first, first, half, 128),
            (from_x, to_x, 2 * TILE + half, 128),
            (from_x, to_x, TILE + half, 128),
        ]
    return [
        ((a, from_y, whole, pl.ds(start, size)), (b, to_y, whole, pl.ds(start, size)))
        for a, b, start, size in parts
    ]


COPIES = sum(len(halo_parts(sx, sy)) for sx, sy in SIDES)


def turn_dense(e, x, y, tile):
    at = TILE * tile
    pile = jnp.concatenate([e[x, y, :, at + 128 : at + 256], e[x, y + 1, :, at : at + 128]], axis=0)
    return pile.T


def fill_inner(e):
    for x, ring, tile in ((1, 0, 0), (4, 5, 2)):
        here, there = TILE * tile, TILE * (2 - tile)
        turned = turn_dense(e, x, 2, tile)
        e[ring, 2, :, there + 128 : there + 256] = turned[0:64]
        e[ring, 3, :, there : there + 128] = turned[64:128]
        for y in (2, 4):
            pile = jnp.concatenate(
                [e[x, y, :, here : here + 128], e[x, y - 1, :, here + 128 : here + 256]], axis=0
            )
            turned = pile.T
            e[ring, y, :, there : there + 128] = turned[0:64]
            e[ring, y - 1, :, there + 128 : there + 256] = turned[64:128]


def fill_outer(e):
    for x, ring, tile in ((1, 0, 0), (4, 5, 2)):
        there = TILE * (2 - tile)
        for y in (0, 4):
            turned = turn_dense(e, x, y, tile)
            e[ring, y, :, there + 128 : there + 256] = turned[0:64]
            e[ring, y + 1, :, there : there + 128] = turned[64:128]
    for x in (2, 3, 4):
        e[x, 0, :, 128:256] = turn_dense(e, x - 1, 0, 2)[0:64]
        e[x, 5, :, 0:128] = turn_dense(e, x - 1, 4, 2)[64:128]


def kernel(
    nx, ny, ham, den, pat, fil, out,
    raw_h, raw_d, pat_row, fil_row, e_h, e_d, e_s, hp, total, result,
    load_sem, store_sem, send_sem, recv_sem,
):
    gx = lax.axis_index("gx")
    gy = lax.axis_index("gy")

    def device(sx, sy):
        return (lax.rem(gx + (sx + nx), nx), lax.rem(gy + (sy + ny), ny))

    load_d = pltpu.make_async_copy(den, raw_d, load_sem.at[0])
    load_h = pltpu.make_async_copy(ham, raw_h, load_sem.at[1])
    load_d.start()
    load_h.start()

    barrier = pltpu.get_barrier_semaphore()
    for sx, sy in SIDES:
        pl.semaphore_signal(barrier, inc=1, device_id=device(sx, sy), device_id_type=MESH)

    row = lax.broadcasted_iota(jnp.int32, (4, LANES), 0)
    lane = lax.broadcasted_iota(jnp.int32, (4, LANES), 1)
    place = ((lane >> 6) & 3) - (row & 1)
    slot = jnp.where((place >= 0) & (place <= 2), 3 * (lane >> 8) + place, 9)
    for x in range(4):
        for source, target in ((pat, pat_row), (fil, fil_row)):
            spread = jnp.zeros((4, LANES), jnp.int32)
            for k in range(9):
                spread = jnp.where(slot == k, source[x, :, k : k + 1], spread)
            target[x] = spread.astype(jnp.float32)

    def spread_strips(raw, e):
        def body(step, carry):
            x = step // 2
            p = step % 2
            gap = jnp.zeros((64, 64), jnp.bfloat16)
            v = raw[x, 2 * p]
            m = pat_row[x, pl.ds(2 * p, 1), :].astype(jnp.bfloat16)
            e[x + 1, 2 * p + 1, :, 0:256] = v[:, 0:256] * m[:, 0:256]
            e[x + 1, 2 * p + 1, :, 256:512] = v[:, 192:448] * m[:, 256:512]
            e[x + 1, 2 * p + 1, :, 512:768] = (
                jnp.concatenate([v[:, 384:576], gap], axis=1) * m[:, 512:768]
            )
            v = raw[x, 2 * p + 1]
            m = pat_row[x, pl.ds(2 * p + 1, 1), :].astype(jnp.bfloat16)
            e[x + 1, 2 * p + 2, :, 0:256] = (
                jnp.concatenate([gap, v[:, 0:192]], axis=1) * m[:, 0:256]
            )
            e[x + 1, 2 * p + 2, :, 256:512] = v[:, 128:384] * m[:, 256:512]
            e[x + 1, 2 * p + 2, :, 512:768] = v[:, 320:576] * m[:, 512:768]
            return carry

        lax.fori_loop(0, 8, body, 0, unroll=8)

    def copies(e, base):
        made = []
        for sx, sy in SIDES:
            for source, target in halo_parts(sx, sy):
                made.append(
                    pltpu.make_async_remote_copy(
                        src_ref=e.at[source],
                        dst_ref=e.at[target],
                        send_sem=send_sem.at[base + len(made)],
                        recv_sem=recv_sem.at[base + len(made)],
                        device_id=device(sx, sy),
                        device_id_type=MESH,
                    )
                )
        return made

    copies_d = copies(e_d, 0)
    copies_h = copies(e_h, COPIES)
    copies_s = copies(e_s, 2 * COPIES)

    load_d.wait()
    spread_strips(raw_d, e_d)
    pl.semaphore_wait(barrier, len(SIDES))
    for copy in copies_d:
        copy.start()
    load_h.wait()
    spread_strips(raw_h, e_h)
    for copy in copies_h:
        copy.start()
    fill_inner(e_d)
    fill_inner(e_h)

    hole = jnp.zeros((64, 128), jnp.bfloat16)

    def product(left, e, x, p, target):
        low = max(target - 1, 0)
        high = min(target + 1, 2)
        rights = []
        for source in range(low, high + 1):
            start = TILE * (target - source + 1)
            first = e[x + source, 2 * p, :, start + 128 : start + 256]
            second = e[x + source, 2 * p + 1, :, start : start + 256]
            third = e[x + source, 2 * p + 2, :, start : start + 256]
            fourth = e[x + source, 2 * p + 3, :, start : start + 128]
            rights.append(jnp.concatenate([first, hole], axis=1))
            rights.append(second)
            rights.append(third)
            rights.append(jnp.concatenate([hole, fourth], axis=1))
        a = left[:, :, TILE * low : TILE * (high + 1)]
        a = a.reshape(128, TILE * (high + 1 - low))
        b = jnp.concatenate(rights, axis=0)
        return jnp.dot(a, b, preferred_element_type=jnp.float32)

    def filter_of(x, p, target):
        even = fil_row[x, pl.ds(2 * p, 1), TILE * target : TILE * (target + 1)]
        odd = fil_row[x, pl.ds(2 * p + 1, 1), TILE * target : TILE * (target + 1)]
        return jnp.concatenate(
            [jnp.broadcast_to(even, (64, TILE)), jnp.broadcast_to(odd, (64, TILE))], axis=0
        )

    def pair(step):
        return step // 2, step % 2

    def hp_body(step, carry):
        x, p = pair(step)
        left = e_h[x + 1, pl.ds(2 * p + 1, 2)]
        for target in range(3):
            value = product(left, e_d, x, p, target) * filter_of(x, p, target)
            hp[x, pl.ds(2 * p, 2), :, TILE * target : TILE * (target + 1)] = value.astype(
                jnp.bfloat16
            ).reshape(2, 64, TILE)
        return carry

    def sum_body(step, carry):
        x, p = pair(step)
        left = e_d[x + 1, pl.ds(2 * p + 1, 2)]
        for target in range(3):
            lanes = slice(TILE * target, TILE * (target + 1))
            turned = product(left, e_h, x, p, target) * filter_of(x, p, target)
            turned = turned.astype(jnp.bfloat16).astype(jnp.float32)
            both = turned + hp[x, pl.ds(2 * p, 2), :, lanes].reshape(128, TILE).astype(jnp.float32)
            total[x, pl.ds(2 * p, 2), :, lanes] = (3.0 * both).reshape(2, 64, TILE)
            e_s[x + 1, pl.ds(2 * p + 1, 2), :, lanes] = both.astype(jnp.bfloat16).reshape(
                2, 64, TILE
            )
        return carry

    def hpp_body(step, carry):
        x, p = pair(step)
        left = hp[x, pl.ds(2 * p, 2)]
        for target in range(3):
            lanes = slice(TILE * target, TILE * (target + 1))
            value = product(left, e_d, x, p, target).reshape(2, 64, TILE)
            total[x, pl.ds(2 * p, 2), :, lanes] = (
                total[x, pl.ds(2 * p, 2), :, lanes] - 2.0 * value
            )
        return carry

    def store(x):
        return pltpu.make_async_copy(result.at[x], out.at[x], store_sem.at[x])

    def last_body(x, carry):
        for p in range(2):
            left = e_d[x + 1, pl.ds(2 * p + 1, 2)]
            parts = []
            for target in range(3):
                lanes = slice(TILE * target, TILE * (target + 1))
                value = product(left, e_s, x, p, target)
                value = total[x, pl.ds(2 * p, 2), :, lanes].reshape(128, TILE) - 2.0 * value
                parts.append((value * filter_of(x, p, target)).astype(jnp.bfloat16))
            result[x, 2 * p] = jnp.concatenate([part[0:64, 0:192] for part in parts], axis=1)
            result[x, 2 * p + 1] = jnp.concatenate(
                [part[64:128, 64:256] for part in parts], axis=1
            )
        return carry

    for copy in copies_d:
        copy.wait_recv()
    fill_outer(e_d)
    lax.fori_loop(0, 8, hp_body, 0, unroll=8)
    for copy in copies_h:
        copy.wait_recv()
    fill_outer(e_h)
    lax.fori_loop(0, 8, sum_body, 0, unroll=8)
    for copy in copies_s:
        copy.start()
    fill_inner(e_s)
    lax.fori_loop(0, 8, hpp_body, 0, unroll=8)
    for copy in copies_s:
        copy.wait_recv()
    fill_outer(e_s)
    for x in range(4):
        last_body(x, 0)
        store(x).start()
    for copy in copies_d + copies_h + copies_s:
        copy.wait_send()
    for x in range(4):
        store(x).wait()


def per_device(nx, ny, hamiltonian, density, block_pattern, filter_mask):
    shape = hamiltonian.shape
    ring = (6, 6, 64, LANES)
    vmem = pl.BlockSpec(memory_space=pltpu.VMEM)
    anywhere = pl.BlockSpec(memory_space=pl.ANY)
    return pl.pallas_call(
        functools.partial(kernel, nx, ny),
        out_shape=jax.ShapeDtypeStruct(shape, jnp.bfloat16),
        in_specs=[anywhere, anywhere, vmem, vmem],
        out_specs=anywhere,
        scratch_shapes=[
            pltpu.VMEM(shape, jnp.bfloat16),
            pltpu.VMEM(shape, jnp.bfloat16),
            pltpu.VMEM((4, 4, LANES), jnp.float32),
            pltpu.VMEM((4, 4, LANES), jnp.float32),
            pltpu.VMEM(ring, jnp.bfloat16),
            pltpu.VMEM(ring, jnp.bfloat16),
            pltpu.VMEM(ring, jnp.bfloat16),
            pltpu.VMEM((4, 4, 64, LANES), jnp.bfloat16),
            pltpu.VMEM((4, 4, 64, LANES), jnp.float32),
            pltpu.VMEM(shape, jnp.bfloat16),
            pltpu.SemaphoreType.DMA((2,)),
            pltpu.SemaphoreType.DMA((4,)),
            pltpu.SemaphoreType.DMA((3 * COPIES,)),
            pltpu.SemaphoreType.DMA((3 * COPIES,)),
        ],
        compiler_params=pltpu.CompilerParams(collective_id=0, has_side_effects=True),
    )(hamiltonian, density, block_pattern, filter_mask)


def solution(mesh):
    return jax.shard_map(
        functools.partial(per_device, mesh.shape["gx"], mesh.shape["gy"]),
        mesh=mesh,
        in_specs=(
            P("gx", "gy", None, None),
            P("gx", "gy", None, None),
            P("gx", "gy", None),
            P("gx", "gy", None),
        ),
        out_specs=P("gx", "gy", None, None),
        check_vma=False,
    )
```

```python
import functools

import jax
import jax.numpy as jnp
from jax import lax
from jax.experimental import pallas as pl
from jax.experimental.pallas import tpu as pltpu
from jax.sharding import PartitionSpec as P

TILE = 256
LANES = 3 * TILE
MESH = pl.DeviceIdType.MESH
SIDES = ((1, 1), (1, -1), (-1, 1), (-1, -1), (0, 1), (0, -1), (1, 0), (-1, 0))


def halo_parts(sx, sy):
    whole = slice(None)
    from_x = {1: pl.ds(4, 1), -1: pl.ds(1, 1), 0: pl.ds(1, 4)}[sx]
    to_x = {1: pl.ds(0, 1), -1: pl.ds(5, 1), 0: pl.ds(1, 4)}[sx]
    from_y = {1: pl.ds(4, 1), -1: pl.ds(1, 1), 0: pl.ds(1, 4)}[sy]
    to_y = {1: pl.ds(0, 1), -1: pl.ds(5, 1), 0: pl.ds(1, 4)}[sy]
    half = 128 if sy == 1 else 0
    if sy == 0:
        rows = (pl.ds(1, 4), pl.ds(2, 1), pl.ds(4, 1))
        parts = [(from_x, to_x, y, y, TILE + (128 if i else 0)) for i, y in enumerate(rows)]
    elif sx != 0:
        parts = [(from_x, to_x, from_y, to_y, TILE + half)]
    else:
        ends = ((pl.ds(1, 1), half), (pl.ds(4, 1), 2 * TILE + half))
        parts = [(x, x, from_y, to_y, start) for x, start in ends]
    return [
        ((a, c, whole, pl.ds(start, 128)), (b, d, whole, pl.ds(start, 128)))
        for a, b, c, d, start in parts
    ]


COPIES = sum(len(halo_parts(sx, sy)) for sx, sy in SIDES) + 2


def pack(e, packed):
    for x in range(4):
        packed[0, x] = jnp.concatenate([e[x + 1, 4, :, 384:448], e[x + 1, 4, :, 640:704]], axis=1)
        packed[1, x] = jnp.concatenate([e[x + 1, 1, :, 320:384], e[x + 1, 1, :, 576:640]], axis=1)


def turn_dense(e, x, y, tile):
    at = TILE * tile
    pile = jnp.concatenate([e[x, y, :, at + 128 : at + 256], e[x, y + 1, :, at : at + 128]], axis=0)
    return pile.T


def fill_inner(e):
    for x, ring, tile in ((1, 0, 0), (4, 5, 2)):
        here, there = TILE * tile, TILE * (2 - tile)
        turned = turn_dense(e, x, 2, tile)
        e[ring, 2, :, there + 128 : there + 256] = turned[0:64]
        e[ring, 3, :, there : there + 128] = turned[64:128]
        for y in (2, 4):
            pile = jnp.concatenate(
                [e[x, y, :, here : here + 128], e[x, y - 1, :, here + 128 : here + 256]], axis=0
            )
            turned = pile.T
            e[ring, y, :, there : there + 128] = turned[0:64]
            e[ring, y - 1, :, there + 128 : there + 256] = turned[64:128]


    gap = jnp.zeros((64, 128), jnp.bfloat16)
    for x in (1, 2, 3, 4):
        for step in (0, 1) if x < 4 else (0,):
            there, here = TILE * (1 + step), TILE * (1 - step)
            pile = jnp.concatenate([gap, e[x + step, 1, :, here : here + 128]], axis=0)
            e[x, 0, :, there + 128 : there + 256] = pile.T[0:64]
            pile = jnp.concatenate([e[x + step, 4, :, here + 128 : here + 256], gap], axis=0)
            e[x, 5, :, there : there + 128] = pile.T[64:128]


def fill_outer(e, packed):
    gap = jnp.zeros((64, 128), jnp.bfloat16)
    for x in (1, 2, 3, 4):
        e[x, 0, :, 384:448] = packed[0, x - 1, :, 0:64]
        e[x, 5, :, 320:384] = packed[1, x - 1, :, 0:64]
        if x < 4:
            e[x, 0, :, 640:704] = packed[0, x - 1, :, 64:128]
            e[x, 5, :, 576:640] = packed[1, x - 1, :, 64:128]
    for ring in (0, 5):
        for y in (1, 3):
            pile = jnp.concatenate([e[ring, y + 1, :, 256:384], gap], axis=0)
            e[ring, y, :, 384:512] = pile.T[64:128]
    for x, ring, tile in ((1, 0, 0), (4, 5, 2)):
        there = TILE * (2 - tile)
        for y in (0, 4):
            turned = turn_dense(e, x, y, tile)
            e[ring, y, :, there + 128 : there + 256] = turned[0:64]
            e[ring, y + 1, :, there : there + 128] = turned[64:128]
    for x in (2, 3, 4):
        e[x, 0, :, 128:256] = turn_dense(e, x - 1, 0, 2)[0:64]
        e[x, 5, :, 0:128] = turn_dense(e, x - 1, 4, 2)[64:128]


def kernel(
    nx, ny, ham, den, pat, fil, out,
    raw_h, raw_d, pat_row, fil_row, e_h, e_d, e_s, hp, total, result, packs, unpacks,
    load_sem, store_sem, send_sem, recv_sem,
):
    gx = lax.axis_index("gx")
    gy = lax.axis_index("gy")

    def device(sx, sy):
        return (lax.rem(gx + (sx + nx), nx), lax.rem(gy + (sy + ny), ny))

    load_d = pltpu.make_async_copy(den, raw_d, load_sem.at[0])
    load_h = pltpu.make_async_copy(ham, raw_h, load_sem.at[1])
    load_d.start()
    load_h.start()

    barrier = pltpu.get_barrier_semaphore()
    for sx, sy in SIDES:
        pl.semaphore_signal(barrier, inc=1, device_id=device(sx, sy), device_id_type=MESH)

    row = lax.broadcasted_iota(jnp.int32, (4, LANES), 0)
    lane = lax.broadcasted_iota(jnp.int32, (4, LANES), 1)
    place = ((lane >> 6) & 3) - (row & 1)
    slot = jnp.where((place >= 0) & (place <= 2), 3 * (lane >> 8) + place, 9)
    for x in range(4):
        for source, target in ((pat, pat_row), (fil, fil_row)):
            spread = jnp.zeros((4, LANES), jnp.int32)
            for k in range(9):
                spread = jnp.where(slot == k, source[x, :, k : k + 1], spread)
            target[x] = spread.astype(jnp.float32)

    def spread_strips(raw, e):
        def body(step, carry):
            x = step // 2
            p = step % 2
            gap = jnp.zeros((64, 64), jnp.bfloat16)
            v = raw[x, 2 * p]
            m = pat_row[x, pl.ds(2 * p, 1), :].astype(jnp.bfloat16)
            e[x + 1, 2 * p + 1, :, 0:256] = v[:, 0:256] * m[:, 0:256]
            e[x + 1, 2 * p + 1, :, 256:512] = v[:, 192:448] * m[:, 256:512]
            e[x + 1, 2 * p + 1, :, 512:768] = (
                jnp.concatenate([v[:, 384:576], gap], axis=1) * m[:, 512:768]
            )
            v = raw[x, 2 * p + 1]
            m = pat_row[x, pl.ds(2 * p + 1, 1), :].astype(jnp.bfloat16)
            e[x + 1, 2 * p + 2, :, 0:256] = (
                jnp.concatenate([gap, v[:, 0:192]], axis=1) * m[:, 0:256]
            )
            e[x + 1, 2 * p + 2, :, 256:512] = v[:, 128:384] * m[:, 256:512]
            e[x + 1, 2 * p + 2, :, 512:768] = v[:, 320:576] * m[:, 512:768]
            return carry

        lax.fori_loop(0, 8, body, 0, unroll=8)

    def copies(e, which):
        base = COPIES * which
        made = []
        for sx, sy in SIDES:
            parts = [(e.at[source], e.at[target]) for source, target in halo_parts(sx, sy)]
            if sx == 0:
                side = 0 if sy == 1 else 1
                parts.append((packs.at[which, side], unpacks.at[which, side]))
            for source, target in parts:
                made.append(
                    pltpu.make_async_remote_copy(
                        src_ref=source,
                        dst_ref=target,
                        send_sem=send_sem.at[base + len(made)],
                        recv_sem=recv_sem.at[base + len(made)],
                        device_id=device(sx, sy),
                        device_id_type=MESH,
                    )
                )
        return made

    copies_d = copies(e_d, 0)
    copies_h = copies(e_h, 1)
    copies_s = copies(e_s, 2)

    load_d.wait()
    spread_strips(raw_d, e_d)
    pack(e_d, packs.at[0])
    pl.semaphore_wait(barrier, len(SIDES))
    for copy in copies_d:
        copy.start()
    load_h.wait()
    spread_strips(raw_h, e_h)
    pack(e_h, packs.at[1])
    for copy in copies_h:
        copy.start()
    fill_inner(e_d)
    fill_inner(e_h)

    hole = jnp.zeros((64, 128), jnp.bfloat16)

    def product(left, e, x, p, target):
        low = max(target - 1, 0)
        high = min(target + 1, 2)
        rights = []
        for source in range(low, high + 1):
            start = TILE * (target - source + 1)
            first = e[x + source, 2 * p, :, start + 128 : start + 256]
            second = e[x + source, 2 * p + 1, :, start : start + 256]
            third = e[x + source, 2 * p + 2, :, start : start + 256]
            fourth = e[x + source, 2 * p + 3, :, start : start + 128]
            rights.append(jnp.concatenate([first, hole], axis=1))
            rights.append(second)
            rights.append(third)
            rights.append(jnp.concatenate([hole, fourth], axis=1))
        a = left[:, :, TILE * low : TILE * (high + 1)]
        a = a.reshape(128, TILE * (high + 1 - low))
        b = jnp.concatenate(rights, axis=0)
        return jnp.dot(a, b, preferred_element_type=jnp.float32)

    def filter_of(x, p, target):
        even = fil_row[x, pl.ds(2 * p, 1), TILE * target : TILE * (target + 1)]
        odd = fil_row[x, pl.ds(2 * p + 1, 1), TILE * target : TILE * (target + 1)]
        return jnp.concatenate(
            [jnp.broadcast_to(even, (64, TILE)), jnp.broadcast_to(odd, (64, TILE))], axis=0
        )

    def pair(step):
        return step // 2, step % 2

    def hp_body(step, carry):
        x, p = pair(step)
        left = e_h[x + 1, pl.ds(2 * p + 1, 2)]
        for target in range(3):
            value = product(left, e_d, x, p, target) * filter_of(x, p, target)
            hp[x, pl.ds(2 * p, 2), :, TILE * target : TILE * (target + 1)] = value.astype(
                jnp.bfloat16
            ).reshape(2, 64, TILE)
        return carry

    def sum_body(step, carry):
        x, p = pair(step)
        left = e_d[x + 1, pl.ds(2 * p + 1, 2)]
        for target in range(3):
            lanes = slice(TILE * target, TILE * (target + 1))
            turned = product(left, e_h, x, p, target) * filter_of(x, p, target)
            turned = turned.astype(jnp.bfloat16).astype(jnp.float32)
            both = turned + hp[x, pl.ds(2 * p, 2), :, lanes].reshape(128, TILE).astype(jnp.float32)
            total[x, pl.ds(2 * p, 2), :, lanes] = (3.0 * both).reshape(2, 64, TILE)
            e_s[x + 1, pl.ds(2 * p + 1, 2), :, lanes] = both.astype(jnp.bfloat16).reshape(
                2, 64, TILE
            )
        return carry

    def hpp_body(step, carry):
        x, p = pair(step)
        left = hp[x, pl.ds(2 * p, 2)]
        for target in range(3):
            lanes = slice(TILE * target, TILE * (target + 1))
            value = product(left, e_d, x, p, target).reshape(2, 64, TILE)
            total[x, pl.ds(2 * p, 2), :, lanes] = (
                total[x, pl.ds(2 * p, 2), :, lanes] - 2.0 * value
            )
        return carry

    def store(x):
        return pltpu.make_async_copy(result.at[x], out.at[x], store_sem.at[x])

    def last_body(x, carry):
        for p in range(2):
            left = e_d[x + 1, pl.ds(2 * p + 1, 2)]
            parts = []
            for target in range(3):
                lanes = slice(TILE * target, TILE * (target + 1))
                value = product(left, e_s, x, p, target)
                value = total[x, pl.ds(2 * p, 2), :, lanes].reshape(128, TILE) - 2.0 * value
                parts.append((value * filter_of(x, p, target)).astype(jnp.bfloat16))
            result[x, 2 * p] = jnp.concatenate([part[0:64, 0:192] for part in parts], axis=1)
            result[x, 2 * p + 1] = jnp.concatenate(
                [part[64:128, 64:256] for part in parts], axis=1
            )
        return carry

    for copy in copies_d:
        copy.wait_recv()
    fill_outer(e_d, unpacks.at[0])
    lax.fori_loop(0, 8, hp_body, 0, unroll=8)
    for copy in copies_h:
        copy.wait_recv()
    fill_outer(e_h, unpacks.at[1])
    for step in (0, 1, 6, 7):
        sum_body(step, 0)
    for copy in copies_s[:4] + copies_s[10:]:
        copy.start()
    for step in (2, 3, 4, 5):
        sum_body(step, 0)
    pack(e_s, packs.at[2])
    for copy in copies_s[4:10]:
        copy.start()
    fill_inner(e_s)
    lax.fori_loop(0, 8, hpp_body, 0, unroll=8)
    for copy in copies_s:
        copy.wait_recv()
    fill_outer(e_s, unpacks.at[2])
    for x in range(4):
        last_body(x, 0)
        store(x).start()
    for copy in copies_d + copies_h + copies_s:
        copy.wait_send()
    for x in range(4):
        store(x).wait()


def per_device(nx, ny, hamiltonian, density, block_pattern, filter_mask):
    shape = hamiltonian.shape
    ring = (6, 6, 64, LANES)
    vmem = pl.BlockSpec(memory_space=pltpu.VMEM)
    anywhere = pl.BlockSpec(memory_space=pl.ANY)
    return pl.pallas_call(
        functools.partial(kernel, nx, ny),
        out_shape=jax.ShapeDtypeStruct(shape, jnp.bfloat16),
        in_specs=[anywhere, anywhere, vmem, vmem],
        out_specs=anywhere,
        scratch_shapes=[
            pltpu.VMEM(shape, jnp.bfloat16),
            pltpu.VMEM(shape, jnp.bfloat16),
            pltpu.VMEM((4, 4, LANES), jnp.float32),
            pltpu.VMEM((4, 4, LANES), jnp.float32),
            pltpu.VMEM(ring, jnp.bfloat16),
            pltpu.VMEM(ring, jnp.bfloat16),
            pltpu.VMEM(ring, jnp.bfloat16),
            pltpu.VMEM((4, 4, 64, LANES), jnp.bfloat16),
            pltpu.VMEM((4, 4, 64, LANES), jnp.float32),
            pltpu.VMEM(shape, jnp.bfloat16),
            pltpu.VMEM((3, 2, 4, 64, 128), jnp.bfloat16),
            pltpu.VMEM((3, 2, 4, 64, 128), jnp.bfloat16),
            pltpu.SemaphoreType.DMA((2,)),
            pltpu.SemaphoreType.DMA((4,)),
            pltpu.SemaphoreType.DMA((3 * COPIES,)),
            pltpu.SemaphoreType.DMA((3 * COPIES,)),
        ],
        compiler_params=pltpu.CompilerParams(collective_id=0, has_side_effects=True),
    )(hamiltonian, density, block_pattern, filter_mask)


def solution(mesh):
    return jax.shard_map(
        functools.partial(per_device, mesh.shape["gx"], mesh.shape["gy"]),
        mesh=mesh,
        in_specs=(
            P("gx", "gy", None, None),
            P("gx", "gy", None, None),
            P("gx", "gy", None),
            P("gx", "gy", None),
        ),
        out_specs=P("gx", "gy", None, None),
        check_vma=False,
    )
```

```python
import functools

import jax
import jax.numpy as jnp
from jax import lax
from jax.experimental import pallas as pl
from jax.experimental.pallas import tpu as pltpu
from jax.sharding import PartitionSpec as P

TILE = 256
LANES = 3 * TILE
MESH = pl.DeviceIdType.MESH
SIDES = ((1, 1), (1, -1), (-1, 1), (-1, -1), (0, 1), (0, -1), (1, 0), (-1, 0))


def halo_parts(sx, sy):
    whole = slice(None)
    from_x = {1: pl.ds(4, 1), -1: pl.ds(1, 1), 0: pl.ds(1, 4)}[sx]
    to_x = {1: pl.ds(0, 1), -1: pl.ds(5, 1), 0: pl.ds(1, 4)}[sx]
    from_y = {1: pl.ds(4, 1), -1: pl.ds(1, 1), 0: pl.ds(1, 4)}[sy]
    to_y = {1: pl.ds(0, 1), -1: pl.ds(5, 1), 0: pl.ds(1, 4)}[sy]
    half = 128 if sy == 1 else 0
    if sy == 0:
        rows = (pl.ds(1, 4), pl.ds(2, 1), pl.ds(4, 1))
        parts = [(from_x, to_x, y, y, TILE + (128 if i else 0)) for i, y in enumerate(rows)]
    elif sx != 0:
        parts = [(from_x, to_x, from_y, to_y, TILE + half)]
    else:
        ends = ((pl.ds(1, 1), half), (pl.ds(4, 1), 2 * TILE + half))
        parts = [(x, x, from_y, to_y, start) for x, start in ends]
    return [
        ((a, c, whole, pl.ds(start, 128)), (b, d, whole, pl.ds(start, 128)))
        for a, b, c, d, start in parts
    ]


COPIES = sum(len(halo_parts(sx, sy)) for sx, sy in SIDES) + 2


def pack(e, packed):
    for x in range(4):
        packed[0, x] = jnp.concatenate([e[x + 1, 4, :, 384:448], e[x + 1, 4, :, 640:704]], axis=1)
        packed[1, x] = jnp.concatenate([e[x + 1, 1, :, 320:384], e[x + 1, 1, :, 576:640]], axis=1)


def turn_dense(e, x, y, tile):
    at = TILE * tile
    pile = jnp.concatenate([e[x, y, :, at + 128 : at + 256], e[x, y + 1, :, at : at + 128]], axis=0)
    return pile.T


def fill_inner(e):
    for x, ring, tile in ((1, 0, 0), (4, 5, 2)):
        here, there = TILE * tile, TILE * (2 - tile)
        turned = turn_dense(e, x, 2, tile)
        e[ring, 2, :, there + 128 : there + 256] = turned[0:64]
        e[ring, 3, :, there : there + 128] = turned[64:128]
        for y in (2, 4):
            pile = jnp.concatenate(
                [e[x, y, :, here : here + 128], e[x, y - 1, :, here + 128 : here + 256]], axis=0
            )
            turned = pile.T
            e[ring, y, :, there : there + 128] = turned[0:64]
            e[ring, y - 1, :, there + 128 : there + 256] = turned[64:128]


    gap = jnp.zeros((64, 128), jnp.bfloat16)
    for x in (1, 2, 3, 4):
        for step in (0, 1) if x < 4 else (0,):
            there, here = TILE * (1 + step), TILE * (1 - step)
            pile = jnp.concatenate([gap, e[x + step, 1, :, here : here + 128]], axis=0)
            e[x, 0, :, there + 128 : there + 256] = pile.T[0:64]
            pile = jnp.concatenate([e[x + step, 4, :, here + 128 : here + 256], gap], axis=0)
            e[x, 5, :, there : there + 128] = pile.T[64:128]


def fill_outer(e, packed):
    gap = jnp.zeros((64, 128), jnp.bfloat16)
    for x in (1, 2, 3, 4):
        e[x, 0, :, 384:448] = packed[0, x - 1, :, 0:64]
        e[x, 5, :, 320:384] = packed[1, x - 1, :, 0:64]
        if x < 4:
            e[x, 0, :, 640:704] = packed[0, x - 1, :, 64:128]
            e[x, 5, :, 576:640] = packed[1, x - 1, :, 64:128]
    for ring in (0, 5):
        for y in (1, 3):
            pile = jnp.concatenate([e[ring, y + 1, :, 256:384], gap], axis=0)
            e[ring, y, :, 384:512] = pile.T[64:128]
    for x, ring, tile in ((1, 0, 0), (4, 5, 2)):
        there = TILE * (2 - tile)
        for y in (0, 4):
            turned = turn_dense(e, x, y, tile)
            e[ring, y, :, there + 128 : there + 256] = turned[0:64]
            e[ring, y + 1, :, there : there + 128] = turned[64:128]
    for x in (2, 3, 4):
        e[x, 0, :, 128:256] = turn_dense(e, x - 1, 0, 2)[0:64]
        e[x, 5, :, 0:128] = turn_dense(e, x - 1, 4, 2)[64:128]


def kernel(
    nx, ny, ham, den, pat, fil, out,
    raw_h, raw_d, pat_row, fil_row, e_h, e_d, e_s, hp, total, packs, unpacks,
    load_sem, send_sem, recv_sem,
):
    gx = lax.axis_index("gx")
    gy = lax.axis_index("gy")

    def device(sx, sy):
        return (lax.rem(gx + (sx + nx), nx), lax.rem(gy + (sy + ny), ny))

    load_d = pltpu.make_async_copy(den, raw_d, load_sem.at[0])
    load_h = pltpu.make_async_copy(ham, raw_h, load_sem.at[1])
    load_d.start()
    load_h.start()

    barrier = pltpu.get_barrier_semaphore()
    for sx, sy in SIDES:
        pl.semaphore_signal(barrier, inc=1, device_id=device(sx, sy), device_id_type=MESH)

    row = lax.broadcasted_iota(jnp.int32, (4, LANES), 0)
    lane = lax.broadcasted_iota(jnp.int32, (4, LANES), 1)
    place = ((lane >> 6) & 3) - (row & 1)
    slot = jnp.where((place >= 0) & (place <= 2), 3 * (lane >> 8) + place, 9)
    for x in range(4):
        for source, target in ((pat, pat_row), (fil, fil_row)):
            spread = jnp.zeros((4, LANES), jnp.int32)
            for k in range(9):
                spread = jnp.where(slot == k, source[x, :, k : k + 1], spread)
            target[x] = spread.astype(jnp.float32)

    def spread_strips(raw, e):
        def body(step, carry):
            x = step // 2
            p = step % 2
            gap = jnp.zeros((64, 64), jnp.bfloat16)
            v = raw[x, 2 * p]
            m = pat_row[x, pl.ds(2 * p, 1), :].astype(jnp.bfloat16)
            e[x + 1, 2 * p + 1, :, 0:256] = v[:, 0:256] * m[:, 0:256]
            e[x + 1, 2 * p + 1, :, 256:512] = v[:, 192:448] * m[:, 256:512]
            e[x + 1, 2 * p + 1, :, 512:768] = (
                jnp.concatenate([v[:, 384:576], gap], axis=1) * m[:, 512:768]
            )
            v = raw[x, 2 * p + 1]
            m = pat_row[x, pl.ds(2 * p + 1, 1), :].astype(jnp.bfloat16)
            e[x + 1, 2 * p + 2, :, 0:256] = (
                jnp.concatenate([gap, v[:, 0:192]], axis=1) * m[:, 0:256]
            )
            e[x + 1, 2 * p + 2, :, 256:512] = v[:, 128:384] * m[:, 256:512]
            e[x + 1, 2 * p + 2, :, 512:768] = v[:, 320:576] * m[:, 512:768]
            return carry

        lax.fori_loop(0, 8, body, 0, unroll=8)

    def copies(e, which):
        base = COPIES * which
        made = []
        for sx, sy in SIDES:
            parts = [(e.at[source], e.at[target]) for source, target in halo_parts(sx, sy)]
            if sx == 0:
                side = 0 if sy == 1 else 1
                parts.append((packs.at[which, side], unpacks.at[which, side]))
            for source, target in parts:
                made.append(
                    pltpu.make_async_remote_copy(
                        src_ref=source,
                        dst_ref=target,
                        send_sem=send_sem.at[base + len(made)],
                        recv_sem=recv_sem.at[base + len(made)],
                        device_id=device(sx, sy),
                        device_id_type=MESH,
                    )
                )
        return made

    copies_d = copies(e_d, 0)
    copies_h = copies(e_h, 1)
    copies_s = copies(e_s, 2)

    load_d.wait()
    spread_strips(raw_d, e_d)
    pack(e_d, packs.at[0])
    pl.semaphore_wait(barrier, len(SIDES))
    for copy in copies_d:
        copy.start()
    load_h.wait()
    spread_strips(raw_h, e_h)
    pack(e_h, packs.at[1])
    for copy in copies_h:
        copy.start()
    fill_inner(e_d)
    fill_inner(e_h)

    hole = jnp.zeros((64, 128), jnp.bfloat16)

    def product(left, e, x, p, target):
        low = max(target - 1, 0)
        high = min(target + 1, 2)
        rights = []
        for source in range(low, high + 1):
            start = TILE * (target - source + 1)
            first = e[x + source, 2 * p, :, start + 128 : start + 256]
            second = e[x + source, 2 * p + 1, :, start : start + 256]
            third = e[x + source, 2 * p + 2, :, start : start + 256]
            fourth = e[x + source, 2 * p + 3, :, start : start + 128]
            rights.append(jnp.concatenate([first, hole], axis=1))
            rights.append(second)
            rights.append(third)
            rights.append(jnp.concatenate([hole, fourth], axis=1))
        a = left[:, :, TILE * low : TILE * (high + 1)]
        a = a.reshape(128, TILE * (high + 1 - low))
        b = jnp.concatenate(rights, axis=0)
        return jnp.dot(a, b, preferred_element_type=jnp.float32)

    def filter_of(x, p, target):
        even = fil_row[x, pl.ds(2 * p, 1), TILE * target : TILE * (target + 1)]
        odd = fil_row[x, pl.ds(2 * p + 1, 1), TILE * target : TILE * (target + 1)]
        return jnp.concatenate(
            [jnp.broadcast_to(even, (64, TILE)), jnp.broadcast_to(odd, (64, TILE))], axis=0
        )

    def pair(step):
        return step // 2, step % 2

    def hp_body(step, carry):
        x, p = pair(step)
        left = e_h[x + 1, pl.ds(2 * p + 1, 2)]
        for target in range(3):
            value = product(left, e_d, x, p, target) * filter_of(x, p, target)
            hp[x, pl.ds(2 * p, 2), :, TILE * target : TILE * (target + 1)] = value.astype(
                jnp.bfloat16
            ).reshape(2, 64, TILE)
        return carry

    def sum_body(step, carry):
        x, p = pair(step)
        left = e_d[x + 1, pl.ds(2 * p + 1, 2)]
        for target in range(3):
            lanes = slice(TILE * target, TILE * (target + 1))
            turned = product(left, e_h, x, p, target) * filter_of(x, p, target)
            turned = turned.astype(jnp.bfloat16).astype(jnp.float32)
            both = turned + hp[x, pl.ds(2 * p, 2), :, lanes].reshape(128, TILE).astype(jnp.float32)
            total[x, pl.ds(2 * p, 2), :, lanes] = (3.0 * both).reshape(2, 64, TILE)
            e_s[x + 1, pl.ds(2 * p + 1, 2), :, lanes] = both.astype(jnp.bfloat16).reshape(
                2, 64, TILE
            )
        return carry

    def hpp_body(step, carry):
        x, p = pair(step)
        left = hp[x, pl.ds(2 * p, 2)]
        for target in range(3):
            lanes = slice(TILE * target, TILE * (target + 1))
            value = product(left, e_d, x, p, target).reshape(2, 64, TILE)
            total[x, pl.ds(2 * p, 2), :, lanes] = (
                total[x, pl.ds(2 * p, 2), :, lanes] - 2.0 * value
            )
        return carry

    def last_body(x, carry):
        for p in range(2):
            left = e_d[x + 1, pl.ds(2 * p + 1, 2)]
            parts = []
            for target in range(3):
                lanes = slice(TILE * target, TILE * (target + 1))
                value = product(left, e_s, x, p, target)
                value = total[x, pl.ds(2 * p, 2), :, lanes].reshape(128, TILE) - 2.0 * value
                parts.append((value * filter_of(x, p, target)).astype(jnp.bfloat16))
            out[x, 2 * p] = jnp.concatenate([part[0:64, 0:192] for part in parts], axis=1)
            out[x, 2 * p + 1] = jnp.concatenate(
                [part[64:128, 64:256] for part in parts], axis=1
            )
        return carry

    for copy in copies_d:
        copy.wait_recv()
    fill_outer(e_d, unpacks.at[0])
    lax.fori_loop(0, 8, hp_body, 0, unroll=8)
    for copy in copies_h:
        copy.wait_recv()
    fill_outer(e_h, unpacks.at[1])
    for step in (0, 1, 6, 7):
        sum_body(step, 0)
    for copy in copies_s[:4] + copies_s[10:]:
        copy.start()
    for step in (2, 3, 4, 5):
        sum_body(step, 0)
    pack(e_s, packs.at[2])
    for copy in copies_s[4:10]:
        copy.start()
    fill_inner(e_s)
    lax.fori_loop(0, 8, hpp_body, 0, unroll=8)
    for copy in copies_s:
        copy.wait_recv()
    fill_outer(e_s, unpacks.at[2])
    for x in range(4):
        last_body(x, 0)
    for copy in copies_d + copies_h + copies_s:
        copy.wait_send()


def per_device(nx, ny, hamiltonian, density, block_pattern, filter_mask):
    shape = hamiltonian.shape
    ring = (6, 6, 64, LANES)
    vmem = pl.BlockSpec(memory_space=pltpu.VMEM)
    anywhere = pl.BlockSpec(memory_space=pl.ANY)
    return pl.pallas_call(
        functools.partial(kernel, nx, ny),
        out_shape=jax.ShapeDtypeStruct(shape, jnp.bfloat16),
        in_specs=[anywhere, anywhere, vmem, vmem],
        out_specs=vmem,
        scratch_shapes=[
            pltpu.VMEM(shape, jnp.bfloat16),
            pltpu.VMEM(shape, jnp.bfloat16),
            pltpu.VMEM((4, 4, LANES), jnp.float32),
            pltpu.VMEM((4, 4, LANES), jnp.float32),
            pltpu.VMEM(ring, jnp.bfloat16),
            pltpu.VMEM(ring, jnp.bfloat16),
            pltpu.VMEM(ring, jnp.bfloat16),
            pltpu.VMEM((4, 4, 64, LANES), jnp.bfloat16),
            pltpu.VMEM((4, 4, 64, LANES), jnp.float32),
            pltpu.VMEM((3, 2, 4, 64, 128), jnp.bfloat16),
            pltpu.VMEM((3, 2, 4, 64, 128), jnp.bfloat16),
            pltpu.SemaphoreType.DMA((2,)),
            pltpu.SemaphoreType.DMA((3 * COPIES,)),
            pltpu.SemaphoreType.DMA((3 * COPIES,)),
        ],
        compiler_params=pltpu.CompilerParams(
            collective_id=0, has_side_effects=True, vmem_limit_bytes=53000 << 10
        ),
    )(hamiltonian, density, block_pattern, filter_mask)


def solution(mesh):
    return jax.shard_map(
        functools.partial(per_device, mesh.shape["gx"], mesh.shape["gy"]),
        mesh=mesh,
        in_specs=(
            P("gx", "gy", None, None),
            P("gx", "gy", None, None),
            P("gx", "gy", None),
            P("gx", "gy", None),
        ),
        out_specs=P("gx", "gy", None, None),
        check_vma=False,
    )
```
